128 devices in a mesh: leaf: 32 (over z, y, core), probe: 4 (over x).
Axes of the slice: x: 4, y: 4, z: 4, core: 2. Of those that a mesh axis runs over, the one named last changes fastest.
Arguments:
- coords: float32 [3, 131072], P(None, 'leaf'), may hold values from 0 to 1
- weights: float32 [131072], P('leaf'), may hold values from 0.01 to 0.1
- omega: bfloat16 [256, 131072], P('probe', 'leaf'), may hold values from -6 to 6
- near_local: int32 [1024, 24], P('leaf'), may hold values from 0 to 1023, as said below
- far_pairs: int32 [2, 8192], P(None, 'leaf'), may hold values from 0 to 1023, as said below
- skel_rows: int32 [1024, 32], P('leaf'), may hold values from 0 to 127, as said below
- parent_interp: bfloat16 [128, 256, 64], P('leaf'), may hold values from -0.375 to 0.375
Outputs:
- near_sample: float32 [256, 131072], P('probe', 'leaf')
- parent_sample: float32 [256, 8192], P('probe', 'leaf')
The draws below stay inside these ranges and needn't reach their ends.
Inputs may be any that keep to these rules, and one draw needn't show every extreme that they name: `near_local`: entry 0 of leaf t's row is t itself; every other entry names a leaf of the same device as t (equal index // 32); repeats may occur. `far_pairs`: column c belongs to device c // 256: its source leaf lies on that device and its target leaf on another device. Of one device's 256 columns at most 16 have targets on any one other device, and one device receives exactly 16 from every other device. `skel_rows`: the 32 numbers of one leaf are distinct.
All inputs are finite; a program needn't handle non-finite values.
Results may differ from the reference program's by a relative error of at most 0.008.
Values may be sent and summed in bfloat16 or wider, within the bound.
A program may use at most 64 MiB of HBM per device.

```python
import math
import jax
import jax.numpy as jnp
from jax import lax

LEAF_PTS = 128
PROBES = 256
SK = 32
SK2 = 64
CHILD = 8
NLOC = 24
CAP = 16
LEAF_DEV = 32
LEAVES = 1024
BOUNDARY_NODES = 131072
PARENTS = 128
REMOTE_DEV = 256
N_LEAF = 32


def draw_near_local(key, part):
    leaf_rows = jnp.arange(LEAVES, dtype=jnp.int32)
    leaf_base = leaf_rows // LEAF_DEV * LEAF_DEV
    others = jax.random.randint(key, (LEAVES, NLOC - 1), 0, LEAF_DEV, dtype=jnp.int32)
    return jnp.concatenate([leaf_rows[:, None], leaf_base[:, None] + others], axis=1)


def draw_far_pairs(key, part):
    device_count = LEAVES // LEAF_DEV
    hot_device = jax.random.randint(jax.random.fold_in(key, 7), (), 0, device_count, dtype=jnp.int32)
    labels = jnp.arange((device_count - 1) * CAP, dtype=jnp.int32) // CAP

    def per_device(device):
        subkey = jax.random.fold_in(key, device + 11)
        key_one, key_two, key_three, key_four = jax.random.split(subkey, 4)
        peer_dev = (device + 1 + labels) % device_count
        scores = jax.random.permutation(key_one, labels.shape[0]).astype(jnp.int32)
        scores = jnp.where(peer_dev == hot_device, scores - labels.shape[0], scores)
        ranked = jnp.argsort(scores, stable=True)[:REMOTE_DEV]
        chosen = jax.random.permutation(key_two, peer_dev[ranked])
        target = chosen * LEAF_DEV + jax.random.randint(key_three, (REMOTE_DEV,), 0, LEAF_DEV, dtype=jnp.int32)
        source = device * LEAF_DEV + jax.random.randint(key_four, (REMOTE_DEV,), 0, LEAF_DEV, dtype=jnp.int32)
        return jnp.stack([source, target])
    pairs = jax.vmap(per_device)(jnp.arange(device_count, dtype=jnp.int32))
    return pairs.transpose(1, 0, 2).reshape(2, device_count * REMOTE_DEV)


def draw_skel_rows(key, part):
    leaf_random_keys = jax.random.split(key, LEAVES)

    def per_leaf(leaf_key):
        return jax.random.permutation(leaf_key, LEAF_PTS)[:SK].astype(jnp.int32)
    return jax.vmap(per_leaf)(leaf_random_keys)


def level_of(key, extent, shards, low, top_value):
    level = 1.0
    for position, parts in shards:
        heights = jax.random.uniform(jax.random.fold_in(jax.random.fold_in(key, 6), position), (parts,), jnp.float32, low / len(shards), top_value / len(shards))
        level = level * jnp.repeat(jnp.exp(heights), extent[position] // parts).reshape((-1,) + (1,) * (len(extent) - 1 - position))
    return level


def normal_values(key, extent, width, reach, pieces=(), kind=jnp.bfloat16):
    entries = jax.random.normal(key, extent, jnp.float32) * width
    if len(pieces) > 0:
        entries = level_of(key, extent, pieces, -0.22, 0.18) * entries
    return jnp.clip(entries, min=-reach, max=reach).astype(kind)


def setup_inputs(seed: int = 0) -> dict:
    seeds = jax.random.split(jax.random.key(seed), 8)
    return {
        "coords": jnp.clip(1.0 * jax.random.uniform(seeds[0], (3, BOUNDARY_NODES), jnp.float32) ** level_of(seeds[0], (3, BOUNDARY_NODES), ((1, 32),), -0.2, 0.2), 0.0, 1.0),
        "weights": jnp.clip(jnp.exp(math.log(0.1) - 2.3025851 * jax.random.uniform(seeds[1], (BOUNDARY_NODES,), jnp.float32) ** level_of(seeds[1], (BOUNDARY_NODES,), ((0, 32),), -0.2, 0.2)), 0.01, 0.1),
        "omega": normal_values(seeds[2], (PROBES, BOUNDARY_NODES), 1.0, 6.0, ((0, 4), (1, 32))),
        "near_local": draw_near_local(jax.random.fold_in(seeds[7], 71), 0),
        "far_pairs": draw_far_pairs(jax.random.fold_in(seeds[7], 71), 0),
        "skel_rows": draw_skel_rows(jax.random.fold_in(seeds[7], 71), 0),
        "parent_interp": normal_values(seeds[6], (PARENTS, CHILD * SK, SK2), (CHILD * SK) ** -0.5, 0.375, ((0, 32),)),
    }


DELTA_SQ = 0.0001
INV_FOUR_PI = 0.07957747154594767

def kernel_block(target_points, source_points, source_weights):
    delta_x = target_points[..., 0, :, None] - source_points[..., 0, None, :]
    delta_y = target_points[..., 1, :, None] - source_points[..., 1, None, :]
    delta_z = target_points[..., 2, :, None] - source_points[..., 2, None, :]
    dist_sq = delta_x * delta_x + delta_y * delta_y + delta_z * delta_z
    values = source_weights[..., None, :] * INV_FOUR_PI * lax.rsqrt(dist_sq + DELTA_SQ)
    return values.astype(jnp.bfloat16)

def reference(coords, weights, omega, near_local, far_pairs, skel_rows, parent_interp):
    leaf_node_coords = coords.reshape(3, LEAVES, LEAF_PTS).transpose(1, 0, 2)
    leaf_weights = weights.reshape(LEAVES, LEAF_PTS)
    leaf_probes = omega.reshape(PROBES, LEAVES, LEAF_PTS).transpose(1, 0, 2)
    block_size = 8

    def local_block(first_leaf):
        targets = lax.dynamic_slice_in_dim(leaf_node_coords, first_leaf, block_size, 0)
        sources = lax.dynamic_slice_in_dim(near_local, first_leaf, block_size, 0)
        kernel = kernel_block(targets[:, None], leaf_node_coords[sources], leaf_weights[sources])
        kernel = lax.optimization_barrier(kernel).astype(jnp.float32)
        return jnp.einsum('bjts,bjps->bpt', kernel, leaf_probes[sources].astype(jnp.float32))
    firsts = jnp.arange(0, LEAVES, block_size, dtype=jnp.int32)
    local_sum = lax.map(local_block, firsts).reshape(LEAVES, PROBES, LEAF_PTS)

    def remote_loop_body(device, total):
        first_pair = (device * REMOTE_DEV).astype(jnp.int32)
        pairs = lax.dynamic_slice_in_dim(far_pairs, first_pair, REMOTE_DEV, 1)
        source = pairs[0]
        target = pairs[1]
        kernel = kernel_block(leaf_node_coords[target], leaf_node_coords[source], leaf_weights[source])
        kernel = lax.optimization_barrier(kernel).astype(jnp.float32)
        partial_rows = jnp.einsum('nts,nps->npt', kernel, leaf_probes[source].astype(jnp.float32))
        partial_rows = lax.optimization_barrier(partial_rows.astype(jnp.bfloat16)).astype(jnp.float32)
        return total.at[target].add(partial_rows)
    far_sum = lax.fori_loop(0, N_LEAF, remote_loop_body, jnp.zeros((LEAVES, PROBES, LEAF_PTS), jnp.float32))
    sampled_block = local_sum + far_sum
    near_sample = sampled_block.transpose(1, 0, 2).reshape(PROBES, BOUNDARY_NODES)
    index_rows = jnp.broadcast_to(skel_rows[:, None, :], (LEAVES, PROBES, SK))
    selected_entries = jnp.take_along_axis(sampled_block, index_rows, axis=2).astype(jnp.bfloat16)
    selected_entries = lax.optimization_barrier(selected_entries).astype(jnp.float32)
    stacked = selected_entries.reshape(PARENTS, CHILD, PROBES, SK).transpose(0, 2, 1, 3).reshape(PARENTS, PROBES, CHILD * SK)
    merged = jnp.einsum('pqc,pck->pqk', stacked, parent_interp.astype(jnp.float32))
    energy = lax.optimization_barrier(jnp.sum(merged * merged, axis=(1, 2)))
    factor = lax.rsqrt(energy / (SK2 * PROBES) + 1e-06)
    parent_sample = (merged * factor[:, None, None]).transpose(1, 0, 2).reshape(PROBES, PARENTS * SK2)
    return (near_sample, parent_sample)
```

```python
import functools
import jax
import jax.numpy as jnp
from jax import lax
from jax.experimental import pallas as pl
from jax.experimental.pallas import tpu as pltpu
from jax.sharding import PartitionSpec as P

PTS = 128
SK = 32
SK2 = 64
CHILD = 8
CAP = 16
DELTA_SQ = 0.0001
INV_FOUR_PI = 0.07957747154594767
BATCH = 8

VMEM = pl.BlockSpec(memory_space=pltpu.VMEM)
SMEM = pl.BlockSpec(memory_space=pltpu.SMEM)
BF = jnp.bfloat16
F32 = jnp.float32


def split3(v):
    a = lax.reduce_precision(v, 8, 7)
    b = lax.reduce_precision(v - a, 8, 7)
    c = lax.reduce_precision(v - a - b, 8, 7)
    return a, b, c


def features(coords):
    c = coords - 0.5
    left, right = [], []
    for d in range(3):
        a1, a2, a3 = split3(c[d])
        b1, b2, b3 = split3(-2.0 * c[d])
        left += [a1, a1, a2, a2, a1, a3]
        right += [b1, b2, b1, b2, b3, b1]
    q = c[0] * c[0] + c[1] * c[1] + c[2] * c[2]
    one = jnp.ones_like(q)
    zero = jnp.zeros_like(q)
    left += [*split3(q), one, one, one]
    right += [one, one, one, *split3(q + DELTA_SQ)]
    left += [zero] * 8
    right += [zero] * 8
    return jnp.stack(left).astype(BF), jnp.stack(right).astype(BF)


def local_kernel(fx_ref, fy_ref, om_ref, cnt_ref, out_ref):
    n = fy_ref.shape[1]
    acc = None
    step = 512
    for j in range(0, n, step):
        d = jnp.dot(fx_ref[...], fy_ref[:, j:j + step], preferred_element_type=F32)
        k = lax.rsqrt(d.astype(BF))
        k0 = k[:PTS] * cnt_ref[0, :, j:j + step]
        k1 = k[PTS:] * cnt_ref[1, :, j:j + step]
        k = jnp.concatenate([k0, k1], axis=0)
        r = lax.dot_general(om_ref[:, j:j + step], k, (((1,), (1,)), ((), ())), preferred_element_type=F32)
        acc = r if acc is None else acc + r
    out_ref[...] = acc


def local_sum(fx, fy, om, cnt):
    n = fy.shape[1]
    rows = om.shape[0]
    return pl.pallas_call(
        local_kernel,
        out_shape=jax.ShapeDtypeStruct((rows, n), F32),
        grid=(n // 256,),
        in_specs=[
            pl.BlockSpec((256, 32), lambda i: (i, 0)),
            pl.BlockSpec((32, n), lambda i: (0, 0)),
            pl.BlockSpec((rows, n), lambda i: (0, 0)),
            pl.BlockSpec((2, 1, n), lambda i: (i, 0, 0)),
        ],
        out_specs=pl.BlockSpec((rows, 256), lambda i: (0, i)),
        cost_estimate=pl.CostEstimate(flops=2 * n * n * (rows + 32), bytes_accessed=4 * rows * n, transcendentals=n * n),
        name="local_sum",
    )(fx, fy, om, cnt)


def far_kernel(code_ref, om_ref, pts_ref, xc_ref, loc_ref, e_ref, near_ref, merged_ref, energy_ref, acc, xb):
    leaf_dev = acc.shape[0]
    slots = code_ref.shape[0]
    for d in range(3):
        for t in range(leaf_dev):
            xb[t, d] = jnp.broadcast_to(xc_ref[t * PTS:(t + 1) * PTS, d:d + 1], (PTS, PTS))
    for t in range(leaf_dev):
        acc[t] = loc_ref[:, t * PTS:(t + 1) * PTS]

    def body(b, carry):
        res = []
        for u in range(BATCH):
            code = code_ref[b * BATCH + u]
            valid = jnp.where(code >= 0, 1.0, 0.0).astype(F32)
            code = jnp.maximum(code, 0)
            s = code // leaf_dev
            t = code % leaf_dev
            p = pts_ref[s]
            dist = None
            for d in range(3):
                dx = xb[t, d] - p[d:d + 1]
                dist = dx * dx if dist is None else dist + dx * dx
            k = lax.rsqrt((dist + DELTA_SQ).astype(BF))
            r = lax.dot_general(om_ref[s], k, (((1,), (1,)), ((), ())), preferred_element_type=F32)
            res.append((t, r * valid))
        for t, r in res:
            acc[t] += r
        return carry

    lax.fori_loop(0, slots // BATCH, body, 0)
    for p in range(leaf_dev // CHILD):
        m = None
        for b in range(CHILD):
            t = p * CHILD + b
            v = acc[t]
            near_ref[:, t * PTS:(t + 1) * PTS] = v
            r = jnp.dot(v.astype(BF), e_ref[t], preferred_element_type=F32)
            m = r if m is None else m + r
        merged_ref[:, p * SK2:(p + 1) * SK2] = m
        energy_ref[p:p + 1] = jnp.broadcast_to(jnp.sum(m * m), (1, PTS))


def far_merge(code, om_all, pts_all, xc, loc, e):
    rows, n = loc.shape
    leaf_dev = n // PTS
    parents = leaf_dev // CHILD
    return pl.pallas_call(
        far_kernel,
        out_shape=(
            jax.ShapeDtypeStruct((rows, n), F32),
            jax.ShapeDtypeStruct((rows, parents * SK2), F32),
            jax.ShapeDtypeStruct((parents, PTS), F32),
        ),
        in_specs=[SMEM] + [VMEM] * 5,
        out_specs=(VMEM, VMEM, VMEM),
        scratch_shapes=[pltpu.VMEM((leaf_dev, rows, PTS), F32), pltpu.VMEM((leaf_dev, 3, PTS, PTS), F32)],
        compiler_params=pltpu.CompilerParams(vmem_limit_bytes=60 * 1024 * 1024),
        name="far_merge",
    )(code, om_all, pts_all, xc, loc, e)


def slot_codes(far_pairs, leaf_dev, n_leaf, offset):
    source = far_pairs[0] - offset
    target = far_pairs[1]
    owner = target // leaf_dev
    hit = (owner[:, None] == jnp.arange(n_leaf, dtype=jnp.int32)[None, :]).astype(jnp.int32)
    ranks = jnp.sum((jnp.cumsum(hit, axis=0) - 1) * hit, axis=1)
    slots = owner * CAP + ranks
    code = far_pairs[0] * leaf_dev + target % leaf_dev
    table = jnp.sum(
        (slots[None, :] == jnp.arange(n_leaf * CAP, dtype=jnp.int32)[:, None]) * (code + 1)[None, :], axis=1
    )
    return (table - 1).reshape(n_leaf, CAP)


def per_device(coords, weights, omega, near_local, far_pairs, skel_rows, parent_interp):
    n_leaf = lax.axis_size("leaf")
    rows, n = omega.shape
    leaf_dev = n // PTS
    offset = lax.axis_index("leaf") * leaf_dev
    leaf_iota = jnp.arange(leaf_dev, dtype=jnp.int32)
    counts = jnp.sum(((near_local - offset)[:, :, None] == leaf_iota).astype(F32), axis=1)
    cnt = jnp.repeat(counts, PTS, axis=1).astype(BF)[:, None]
    omw = (omega.astype(F32) * (weights * INV_FOUR_PI)[None]).astype(BF)
    om_leaf = omw.reshape(rows, leaf_dev, PTS).transpose(1, 0, 2)
    pts = coords.reshape(3, leaf_dev, PTS).transpose(1, 0, 2)
    left, right = features(coords)
    codes = slot_codes(far_pairs, leaf_dev, n_leaf, offset)
    codes = lax.all_to_all(codes, "leaf", split_axis=0, concat_axis=0, tiled=True)
    om_all = lax.all_gather(om_leaf, "leaf", axis=0, tiled=True)
    pts_all = lax.all_gather(pts, "leaf", axis=0, tiled=True)
    loc = local_sum(left.T, right, omw, cnt)
    pick = (jnp.arange(PTS, dtype=jnp.int32)[None, :, None] == skel_rows[:, None, :]).astype(BF)
    e = jnp.einsum("tir,trk->tik", pick, parent_interp.reshape(leaf_dev, SK, SK2), preferred_element_type=F32).astype(BF)
    near, merged, energy = far_merge(codes.reshape(-1), om_all, pts_all, coords.T, loc, e)
    energy = lax.psum(energy[:, 0], "probe")
    factor = lax.rsqrt(energy / (SK2 * rows * lax.axis_size("probe")) + 1e-06)
    return near, merged * jnp.repeat(factor, SK2)[None]


def solution(mesh):
    return jax.shard_map(
        per_device,
        mesh=mesh,
        in_specs=(
            P(None, "leaf"),
            P("leaf"),
            P("probe", "leaf"),
            P("leaf", None),
            P(None, "leaf"),
            P("leaf", None),
            P("leaf", None, None),
        ),
        out_specs=(P("probe", "leaf"), P("probe", "leaf")),
        check_vma=False,
    )
```

```python
import jax
import jax.numpy as jnp
from jax import lax
from jax.experimental import pallas as pl
from jax.experimental.pallas import tpu as pltpu
from jax.sharding import PartitionSpec as P

PTS = 128
SK = 32
SK2 = 64
CHILD = 8
CAP = 16
LEAF_DEV = 32
RING = 16
NSUB = 4
JSTEP = 512
DELTA_SQ = 0.0001
INV_FOUR_PI = 0.07957747154594767

VMEM = pl.BlockSpec(memory_space=pltpu.VMEM)
SMEM = pl.BlockSpec(memory_space=pltpu.SMEM)
ANY = pl.BlockSpec(memory_space=pl.ANY)
MESH = pl.DeviceIdType.MESH
BF = jnp.bfloat16
F32 = jnp.float32
I32 = jnp.int32


def ring_position(leaf):
    z, y, core = leaf // 8, (leaf // 2) % 4, leaf % 2
    return 4 * (y * (1 - core) + z * core) + (y + z) % 4


def ring_device(core, position):
    p = (position + 2 * RING) % RING
    r, c = p // 4, p % 4
    o = (c - r + 4) % 4
    y = r * (1 - core) + o * core
    z = o * (1 - core) + r * core
    return (z * 4 + y) * 2 + core


def split3(v):
    a = v.astype(BF).astype(F32)
    b = (v - a).astype(BF).astype(F32)
    c = (v - a - b).astype(BF).astype(F32)
    return a, b, c


def kernel_body(
    om_ref, coords_ref, w_ref, near_ids_ref, far_pairs_ref, skel_ref, interp_ref, near_ref, parent_ref, *s
):
    bufs, pbufs = list(s[:16]), list(s[16:32])
    mb, pmb = list(s[32:48]), list(s[48:64])
    tb, ptb = list(s[64:80]), list(s[80:96])
    (om_flat, rec, last, tile, srec, slast, fx, fy, cntx, xb, chain, et, merged, energy, got,
     ssem, rsem, pssem, prsem, xssem, xrsem, csem, lsem, essem, ersem) = s[96:]
    me = lax.axis_index("leaf")
    x = lax.axis_index("probe")
    n_probe = lax.axis_size("probe")
    core = me % 2
    pos = ring_position(me)
    nxt, prv = ring_device(core, pos + 1), ring_device(core, pos - 1)
    partner = me + 1 - 2 * core
    rows, n = om_ref.shape
    per_sub = LEAF_DEV // NSUB
    per_probe = LEAF_DEV // n_probe
    barrier = pltpu.get_barrier_semaphore()
    for dev in (nxt, prv, partner):
        pl.semaphore_signal(barrier, inc=1, device_id=(dev, x), device_id_type=MESH)
    for k in range(1, n_probe):
        pl.semaphore_signal(barrier, inc=1, device_id=(me, (x + k) % n_probe), device_id_type=MESH)
    for t in range(LEAF_DEV):
        sl = slice(t * PTS, (t + 1) * PTS)
        v = (om_ref[:, sl].astype(F32) * (w_ref[:, sl] * INV_FOUR_PI)).astype(BF)
        bufs[0][t] = v
        om_flat[:, sl] = v
        mb[0][t] = coords_ref[:, sl]
    pl.semaphore_wait(barrier, 3 + n_probe - 1)

    def remote(src, dst, ss, rs, dev, probe=None):
        return pltpu.make_async_remote_copy(
            src_ref=src, dst_ref=dst, send_sem=ss, recv_sem=rs,
            device_id=(dev, x if probe is None else probe), device_id_type=MESH,
        )

    def ends(d, way):
        return (d, d + 1, nxt) if way == 0 else ((RING - d) % RING, RING - d - 1, prv)

    def ring_om(d, sub, way):
        i, j, dev = ends(d, way)
        sl = pl.ds(sub * per_sub, per_sub)
        return remote(bufs[i].at[sl], bufs[j].at[sl], ssem.at[way, d, sub], rsem.at[way, d, sub], dev)

    def ring_pts(d, way):
        i, j, dev = ends(d, way)
        sl = pl.ds(x * per_probe, per_probe)
        return remote(mb[i].at[sl], mb[j].at[sl], ssem.at[way, d, NSUB], rsem.at[way, d, NSUB], dev)

    def probe_pts(i, k):
        sl = pl.ds(x * per_probe, per_probe)
        return remote(mb[i].at[sl], mb[i].at[sl], xssem.at[i, k - 1], xrsem.at[i, k - 1], me, (x + k) % n_probe)

    def probe_pts_in(i, k):
        sl = pl.ds(((x + n_probe - k) % n_probe) * per_probe, per_probe)
        return remote(mb[i].at[sl], mb[i].at[sl], xssem.at[i, k - 1], xrsem.at[i, k - 1], me, (x + k) % n_probe)

    def ring_tab(d, way):
        i, j, dev = ends(d, way)
        return remote(tb[i], tb[j], ssem.at[way, d, NSUB + 1], rsem.at[way, d, NSUB + 1], dev)

    def pair_om(i, sub):
        sl = pl.ds(sub * per_sub, per_sub)
        return remote(bufs[i].at[sl], pbufs[i].at[sl], pssem.at[i, sub], prsem.at[i, sub], partner)

    def pair_pts(i):
        return remote(mb[i], pmb[i], pssem.at[i, NSUB], prsem.at[i, NSUB], partner)

    def pair_tab(i):
        return remote(tb[i], ptb[i], pssem.at[i, NSUB + 1], prsem.at[i, NSUB + 1], partner)

    def subs(d, way):
        if d < 7:
            return range(NSUB)
        return range(NSUB // 2) if way == 0 else range(NSUB // 2, NSUB)

    def small(d, way):
        return d < 7 or way == 0

    def make_table():
        def column(row):
            return jnp.concatenate(
                [jnp.broadcast_to(row[:, h * PTS:(h + 1) * PTS], (PTS, PTS)).T for h in range(row.shape[1] // PTS)], axis=0
            )

        src = lax.bitwise_and(far_pairs_ref[0:1, :], LEAF_DEV - 1)
        tgt = far_pairs_ref[1:2, :]
        m = tgt.shape[1]
        tcol = column(tgt)
        rank = []
        for h in range(m // PTS):
            trow = jnp.broadcast_to(tgt[:, h * PTS:(h + 1) * PTS], (m, PTS))
            sub_i = lax.broadcasted_iota(I32, (m, PTS), 0)
            lane_i = lax.broadcasted_iota(I32, (m, PTS), 1) + h * PTS
            same = lax.shift_right_logical(trow, 5) == lax.shift_right_logical(tcol, 5)
            before = (tcol < trow) | ((tcol == trow) & (sub_i < lane_i))
            rank.append(jnp.sum((same & before).astype(I32), axis=0, keepdims=True))
        rank = jnp.concatenate(rank, axis=1)
        slot = column(lax.shift_right_logical(tgt, 5) * CAP + rank)
        code = column(src * LEAF_DEV + lax.bitwise_and(tgt, LEAF_DEV - 1) + 1)
        lane_i = lax.broadcasted_iota(I32, (m, PTS), 1)
        for r in range(tb[0].shape[0]):
            hit = slot == lane_i + r * PTS
            tb[0][r:r + 1, :] = jnp.sum(jnp.where(hit, code, 0), axis=0, keepdims=True) - 1

    def link(c, tab):
        row = tab[pl.ds(me // 8, 1), :]
        tile[...] = jnp.broadcast_to(row, (PTS, PTS)).T
        code = tile[pl.ds((me % 8) * CAP, CAP), :]
        sub_i = lax.broadcasted_iota(I32, (CAP, PTS), 0)
        lane_i = lax.broadcasted_iota(I32, (CAP, PTS), 1)
        valid = code >= 0
        target = jnp.where(valid, lax.bitwise_and(code, LEAF_DEV - 1), PTS)
        hit = target == lane_i
        run = valid & (sub_i > 0) & (target == pltpu.roll(target, 1, 0))
        prev = jnp.sum(jnp.where(hit, jnp.broadcast_to(last[...], (CAP, PTS)), 0), axis=1, keepdims=True)
        prev = jnp.where(run, 0, prev)
        word = jnp.where(valid, code, 0) + prev * 1024 + run.astype(I32) * (1024 * 1024)
        rec[c] = jnp.sum(jnp.where(sub_i == lane_i, word, 0), axis=0, keepdims=True)
        new = jnp.max(jnp.where(hit, sub_i + c * CAP, 0), axis=0, keepdims=True)
        last[...] = jnp.where(new > 0, new, last[...])

    def link_out(c):
        return pltpu.make_async_copy(rec.at[c], srec.at[c], csem.at[c])

    def far_chunk(c, om, pts):
        def body(b, full):
            for u in range(8):
                k = b * 8 + u
                word = srec[c, 0, k]
                src = lax.bitwise_and(lax.shift_right_logical(word, 5), LEAF_DEV - 1)
                t = lax.bitwise_and(word, LEAF_DEV - 1)
                prev = lax.bitwise_and(lax.shift_right_logical(word, 10), 1023)
                run = lax.shift_right_logical(word, 20).astype(F32)
                p = pts[src]
                dist = None
                for d in range(3):
                    dx = xb[t, d] - p[d:d + 1]
                    dist = dx * dx if dist is None else dist + dx * dx
                kern = lax.rsqrt((dist + DELTA_SQ).astype(BF))
                r = lax.dot_general(om[src], kern, (((1,), (1,)), ((), ())), preferred_element_type=F32)
                full = r + chain[prev] + full * run
                chain[c * CAP + k] = full
            return full

        lax.fori_loop(0, CAP // 8, body, jnp.zeros((rows, PTS), F32))

    def prepare():
        lane8 = lax.broadcasted_iota(I32, (8, PTS), 0)

        def leaf(t, carry):
            sl = pl.ds(pl.multiple_of(t * PTS, PTS), PTS)
            raw = mb[0][t]
            for d in range(3):
                xb[t, d] = jnp.broadcast_to(raw[d:d + 1], (PTS, PTS)).T
            c = raw - 0.5
            cx, cy, cz = c[0:1], c[1:2], c[2:3]
            q = cx * cx + cy * cy + cz * cz

            def stack(r0, r1, r2, r3, r4):
                v = jnp.where(lane8 == 0, r0, 0.0)
                v = jnp.where(lane8 == 1, r1, v)
                v = jnp.where(lane8 == 2, r2, v)
                v = jnp.where(lane8 == 3, r3, v)
                return jnp.where(lane8 == 4, r4, v)

            a1, a2, a3 = split3(stack(cx, cy, cz, q, 1.0))
            b1, b2, b3 = split3(stack(-2.0 * cx, -2.0 * cy, -2.0 * cz, 1.0, q + DELTA_SQ))
            left = jnp.concatenate([a1, a1, a2, a2, a1, a3], axis=0)
            fx[sl, :] = left.T.astype(BF)
            fy[:, sl] = jnp.concatenate([b1, b2, b1, b2, b3, b1], axis=0).astype(BF)
            return carry

        lax.fori_loop(0, LEAF_DEV, leaf, 0)
        ids = near_ids_ref[...] - me * LEAF_DEV
        sub_i = lax.broadcasted_iota(I32, (LEAF_DEV, LEAF_DEV), 0)
        cnt = jnp.zeros((LEAF_DEV, LEAF_DEV), F32)
        for e in range(ids.shape[0]):
            cnt = cnt + (ids[e:e + 1, :] == sub_i).astype(F32)
        cnt = cnt.T
        for t in range(LEAF_DEV):
            cntx[:, t * PTS:(t + 1) * PTS] = jnp.broadcast_to(cnt[:, t:t + 1], (LEAF_DEV, PTS))

    def prepare_merge():
        for t in range(LEAF_DEV):
            pick = (lax.broadcasted_iota(I32, (PTS, SK), 0) == skel_ref[t:t + 1, :]).astype(F32).astype(BF)
            part = interp_ref[t // CHILD, :, (t % CHILD) * SK:(t % CHILD + 1) * SK]
            et[t] = lax.dot_general(part, pick, (((1,), (1,)), ((), ())), preferred_element_type=F32).astype(BF)

    def near_part(strip, half):
        here = pl.ds(pl.multiple_of(strip * 256, 256), 256)
        acc = None
        for j in range(half * n // 2, (half + 1) * n // 2, JSTEP):
            d = jnp.dot(fx[here, :], fy[:, j:j + JSTEP], preferred_element_type=F32)
            k = lax.rsqrt(d.astype(BF))
            c0 = cntx[pl.ds(2 * strip, 1), j:j + JSTEP].astype(BF)
            c1 = cntx[pl.ds(2 * strip + 1, 1), j:j + JSTEP].astype(BF)
            k = jnp.concatenate([k[:PTS] * c0, k[PTS:] * c1], axis=0)
            r = lax.dot_general(om_flat[:, j:j + JSTEP], k, (((1,), (1,)), ((), ())), preferred_element_type=F32)
            acc = r if acc is None else acc + r
        if half == 0:
            near_ref[:, here] = acc
        else:
            near_ref[:, here] += acc

    near_work = [(st, h) for st in range(LEAF_DEV // 2) for h in range(2)]
    far_ready = []

    def do_near(m):
        for a, b in near_work[:m]:
            near_part(a, b)
        del near_work[:m]

    def do_far(m):
        for _ in range(min(m, len(far_ready))):
            kind, i = far_ready.pop(0)
            c = i + kind * RING
            if kind:
                for sub in range(NSUB):
                    pair_om(i, sub).wait_recv()
                pair_pts(i).wait_recv()
            link_out(c).wait()
            far_chunk(c, (pbufs if kind else bufs)[i], (pmb if kind else mb)[i])

    for way in (0, 1):
        ring_pts(0, way).start()
        ring_om(0, 0, way).start()
    make_table()
    for sub in range(1, NSUB):
        for way in (0, 1):
            ring_om(0, sub, way).start()
    pair_pts(0).start()
    for sub in range(NSUB):
        pair_om(0, sub).start()
    last[...] = jnp.zeros((1, PTS), I32)
    chain[0] = jnp.zeros((rows, PTS), F32)
    prepare()
    for way in (0, 1):
        ring_tab(0, way).start()
    pair_tab(0).start()
    do_near(1)

    def links(chunks):
        for kind, i in chunks:
            if kind:
                pair_tab(i).wait_recv()
            link(i + kind * RING, (ptb if kind else tb)[i])
        return chunks

    for d in range(8):
        ways = [way for way in (0, 1) if small(d, way)]
        for way in ways:
            i = ends(d, way)[1]
            ring_pts(d, way).wait_recv()
            if d < 7 and small(d + 1, way):
                ring_pts(d + 1, way).start()
            for k in range(1, n_probe):
                probe_pts(i, k).start()

        def tables():
            for way in ways:
                i = ends(d, way)[1]
                ring_tab(d, way).wait_recv()
                if d < 7 and small(d + 1, way):
                    ring_tab(d + 1, way).start()
                pair_tab(i).start()

        def points():
            for way in ways:
                i = ends(d, way)[1]
                for k in range(1, n_probe):
                    probe_pts_in(i, k).wait_recv()
                pair_pts(i).start()

        arrived = [(kind, ends(d, way)[1]) for kind in (0, 1) for way in ways]
        if d == 0:
            arrived = [(1, 0)] + arrived
        for sub in range(NSUB):
            for way in (0, 1):
                if sub not in subs(d, way):
                    continue
                i = ends(d, way)[1]
                ring_om(d, sub, way).wait_recv()
                if d < 7 and sub in subs(d + 1, way):
                    ring_om(d + 1, sub, way).start()
                pair_om(i, sub).start()
            if sub == 0:
                tables()
            if d < 7:
                do_near(2 if d == 0 else 1)
                do_far(1)
            if sub == 1:
                points()
        if d == 7:
            links(arrived)
            do_far(1)
            for kind, i in arrived:
                link_out(i + kind * RING).start()
            do_far(len(far_ready))
        else:
            links(arrived)
            do_near(1)
            for kind, i in arrived:
                link_out(i + kind * RING).start()
            if d == 0:
                prepare_merge()
        far_ready += arrived
    last_out = pltpu.make_async_copy(last, slast, lsem)
    last_out.start()
    do_near(len(near_work))
    do_far(len(far_ready))
    last_out.wait()

    for p in range(LEAF_DEV // CHILD):
        m = None
        for t in range(p * CHILD, (p + 1) * CHILD):
            sl = slice(t * PTS, (t + 1) * PTS)
            v = near_ref[:, sl] + chain[slast[0, t]]
            near_ref[:, sl] = v
            r = lax.dot_general(v.astype(BF), et[t], (((1,), (1,)), ((), ())), preferred_element_type=F32)
            m = r if m is None else m + r
        merged[p] = m
        energy[p:p + 1] = jnp.broadcast_to(jnp.sum(m * m), (1, PTS))

    for d in range(8):
        for way in (0, 1):
            for sub in subs(d, way):
                ring_om(d, sub, way).wait_send()
            if small(d, way):
                i = ends(d, way)[1]
                ring_tab(d, way).wait_send()
                ring_pts(d, way).wait_send()
                for k in range(1, n_probe):
                    probe_pts(i, k).wait_send()
    copies = [
        remote(energy, got.at[k - 1], essem.at[k - 1], ersem.at[k - 1], me, (x + k) % n_probe) for k in range(1, n_probe)
    ]
    for cp in copies:
        cp.start()
    for i in range(RING):
        for sub in range(NSUB):
            pair_om(i, sub).wait_send()
        pair_tab(i).wait_send()
        pair_pts(i).wait_send()
    for cp in copies:
        cp.wait()
    total = energy[...]
    for k in range(n_probe - 1):
        total = total + got[k]
    factor = lax.rsqrt(total / (SK2 * rows * n_probe) + 1e-06)
    for p in range(LEAF_DEV // CHILD):
        parent_ref[:, p * SK2:(p + 1) * SK2] = merged[p] * factor[p:p + 1, :SK2]


def sample(om, coords, w, near_ids, far_pairs, skel, interp):
    rows, n = om.shape
    n_probe = lax.axis_size("probe")
    parents = LEAF_DEV // CHILD
    slots = 2 * RING * CAP
    dma = pltpu.SemaphoreType.DMA
    return pl.pallas_call(
        kernel_body,
        out_shape=(
            jax.ShapeDtypeStruct((rows, n), F32),
            jax.ShapeDtypeStruct((rows, parents * SK2), F32),
        ),
        in_specs=[VMEM] * 7,
        out_specs=(VMEM, VMEM),
        scratch_shapes=[pltpu.VMEM((LEAF_DEV, rows, PTS), BF)] * 32
        + [pltpu.VMEM((LEAF_DEV, 3, PTS), F32)] * 32
        + [pltpu.VMEM((RING * 2 * CAP // PTS, PTS), I32)] * 32
        + [
            pltpu.VMEM((rows, n), BF),
            pltpu.VMEM((2 * RING, 1, PTS), I32),
            pltpu.VMEM((1, PTS), I32),
            pltpu.VMEM((PTS, PTS), I32),
            pltpu.SMEM((2 * RING, 1, PTS), I32),
            pltpu.SMEM((1, PTS), I32),
            pltpu.VMEM((n, 48), BF),
            pltpu.VMEM((48, n), BF),
            pltpu.VMEM((LEAF_DEV, n), F32),
            pltpu.VMEM((LEAF_DEV, 3, PTS, PTS), F32),
            pltpu.VMEM((slots, rows, PTS), F32),
            pltpu.VMEM((LEAF_DEV, SK2, PTS), BF),
            pltpu.VMEM((parents, rows, SK2), F32),
            pltpu.VMEM((parents, PTS), F32),
            pltpu.VMEM((n_probe - 1, parents, PTS), F32),
            dma((2, 8, NSUB + 2)),
            dma((2, 8, NSUB + 2)),
            dma((RING, NSUB + 2)),
            dma((RING, NSUB + 2)),
            dma((RING, n_probe - 1)),
            dma((RING, n_probe - 1)),
            dma((2 * RING,)),
            dma(()),
            dma((n_probe - 1,)),
            dma((n_probe - 1,)),
        ],
        compiler_params=pltpu.CompilerParams(
            collective_id=0, has_side_effects=True, vmem_limit_bytes=62 * 1024 * 1024
        ),
        name="sample",
    )(om, coords, w, near_ids, far_pairs, skel, interp)


def per_device(coords, weights, omega, near_local, far_pairs, skel_rows, parent_interp):
    return sample(
        omega, coords, weights.reshape(1, -1), near_local.T, far_pairs, skel_rows, parent_interp.transpose(0, 2, 1)
    )


def solution(mesh):
    return jax.shard_map(
        per_device,
        mesh=mesh,
        in_specs=(
            P(None, "leaf"),
            P("leaf"),
            P("probe", "leaf"),
            P("leaf", None),
            P(None, "leaf"),
            P("leaf", None),
            P("leaf", None, None),
        ),
        out_specs=(P("probe", "leaf"), P("probe", "leaf")),
        check_vma=False,
    )
```

```python
import jax
import jax.numpy as jnp
from jax import lax
from jax.experimental import pallas as pl
from jax.experimental.pallas import tpu as pltpu
from jax.sharding import PartitionSpec as P

PTS = 128
SK = 32
SK2 = 64
CHILD = 8
CAP = 16
LEAF_DEV = 32
RING = 16
NSUB = 2
JSTEP = 512
DELTA_SQ = 0.0001
INV_FOUR_PI = 0.07957747154594767

VMEM = pl.BlockSpec(memory_space=pltpu.VMEM)
SMEM = pl.BlockSpec(memory_space=pltpu.SMEM)
ANY = pl.BlockSpec(memory_space=pl.ANY)
MESH = pl.DeviceIdType.MESH
BF = jnp.bfloat16
F32 = jnp.float32
I32 = jnp.int32


def ring_position(leaf):
    z, y, core = leaf // 8, (leaf // 2) % 4, leaf % 2
    return 4 * (y * (1 - core) + z * core) + (y + z) % 4


def ring_device(core, position):
    p = (position + 2 * RING) % RING
    r, c = p // 4, p % 4
    o = (c - r + 4) % 4
    y = r * (1 - core) + o * core
    z = o * (1 - core) + r * core
    return (z * 4 + y) * 2 + core


def split3(v):
    a = v.astype(BF).astype(F32)
    b = (v - a).astype(BF).astype(F32)
    c = (v - a - b).astype(BF).astype(F32)
    return a, b, c


def kernel_body(
    om_ref, coords_ref, w_ref, near_ids_ref, far_pairs_ref, skel_ref, interp_ref, near_ref, parent_ref, *s
):
    bufs, pbufs = list(s[:16]), list(s[16:32])
    mb, pmb = list(s[32:48]), list(s[48:64])
    tb, ptb = list(s[64:80]), list(s[80:96])
    (om_flat, rec, last, tile, srec, slast, fx, fy, cntx, xb, chain, et, merged, energy, got,
     ssem, rsem, pssem, prsem, xssem, xrsem, csem, lsem, essem, ersem) = s[96:]
    me = lax.axis_index("leaf")
    x = lax.axis_index("probe")
    n_probe = lax.axis_size("probe")
    core = me % 2
    pos = ring_position(me)
    nxt, prv = ring_device(core, pos + 1), ring_device(core, pos - 1)
    partner = me + 1 - 2 * core
    rows, n = om_ref.shape
    per_sub = LEAF_DEV // NSUB
    per_probe = LEAF_DEV // n_probe
    barrier = pltpu.get_barrier_semaphore()
    for dev in (nxt, prv, partner):
        pl.semaphore_signal(barrier, inc=1, device_id=(dev, x), device_id_type=MESH)
    for k in range(1, n_probe):
        pl.semaphore_signal(barrier, inc=1, device_id=(me, (x + k) % n_probe), device_id_type=MESH)
    for t in range(LEAF_DEV):
        sl = slice(t * PTS, (t + 1) * PTS)
        v = (om_ref[:, sl].astype(F32) * (w_ref[:, sl] * INV_FOUR_PI)).astype(BF)
        bufs[0][t] = v
        om_flat[:, sl] = v
        mb[0][t] = coords_ref[:, sl]
    pl.semaphore_wait(barrier, 3 + n_probe - 1)

    def remote(src, dst, ss, rs, dev, probe=None):
        return pltpu.make_async_remote_copy(
            src_ref=src, dst_ref=dst, send_sem=ss, recv_sem=rs,
            device_id=(dev, x if probe is None else probe), device_id_type=MESH,
        )

    def ends(d, way):
        return (d, d + 1, nxt) if way == 0 else ((RING - d) % RING, RING - d - 1, prv)

    def ring_om(d, sub, way):
        i, j, dev = ends(d, way)
        sl = pl.ds(sub * per_sub, per_sub)
        return remote(bufs[i].at[sl], bufs[j].at[sl], ssem.at[way, d, sub], rsem.at[way, d, sub], dev)

    def ring_pts(d, way):
        i, j, dev = ends(d, way)
        sl = pl.ds(x * per_probe, per_probe)
        return remote(mb[i].at[sl], mb[j].at[sl], ssem.at[way, d, NSUB], rsem.at[way, d, NSUB], dev)

    def probe_pts(i, k):
        sl = pl.ds(x * per_probe, per_probe)
        return remote(mb[i].at[sl], mb[i].at[sl], xssem.at[i, k - 1], xrsem.at[i, k - 1], me, (x + k) % n_probe)

    def probe_pts_in(i, k):
        sl = pl.ds(((x + n_probe - k) % n_probe) * per_probe, per_probe)
        return remote(mb[i].at[sl], mb[i].at[sl], xssem.at[i, k - 1], xrsem.at[i, k - 1], me, (x + k) % n_probe)

    def ring_tab(d, way):
        i, j, dev = ends(d, way)
        return remote(tb[i], tb[j], ssem.at[way, d, NSUB + 1], rsem.at[way, d, NSUB + 1], dev)

    def pair_om(i):
        return remote(bufs[i], pbufs[i], pssem.at[i, 0], prsem.at[i, 0], partner)

    def pair_pts(i):
        return remote(mb[i], pmb[i], pssem.at[i, NSUB], prsem.at[i, NSUB], partner)

    def pair_tab(i):
        return remote(tb[i], ptb[i], pssem.at[i, NSUB + 1], prsem.at[i, NSUB + 1], partner)

    def subs(d, way):
        if d < 7:
            return range(NSUB)
        return range(NSUB // 2) if way == 0 else range(NSUB // 2, NSUB)

    def small(d, way):
        return d < 7 or way == 0

    def make_table():
        def column(row):
            return jnp.concatenate(
                [jnp.broadcast_to(row[:, h * PTS:(h + 1) * PTS], (PTS, PTS)).T for h in range(row.shape[1] // PTS)], axis=0
            )

        src = lax.bitwise_and(far_pairs_ref[0:1, :], LEAF_DEV - 1)
        tgt = far_pairs_ref[1:2, :]
        m = tgt.shape[1]
        tcol = column(tgt)
        rank = []
        for h in range(m // PTS):
            trow = jnp.broadcast_to(tgt[:, h * PTS:(h + 1) * PTS], (m, PTS))
            sub_i = lax.broadcasted_iota(I32, (m, PTS), 0)
            lane_i = lax.broadcasted_iota(I32, (m, PTS), 1) + h * PTS
            same = lax.shift_right_logical(trow, 5) == lax.shift_right_logical(tcol, 5)
            before = (tcol < trow) | ((tcol == trow) & (sub_i < lane_i))
            rank.append(jnp.sum((same & before).astype(I32), axis=0, keepdims=True))
        rank = jnp.concatenate(rank, axis=1)
        slot = column(lax.shift_right_logical(tgt, 5) * CAP + rank)
        code = column(src * LEAF_DEV + lax.bitwise_and(tgt, LEAF_DEV - 1) + 1)
        lane_i = lax.broadcasted_iota(I32, (m, PTS), 1)
        for r in range(tb[0].shape[0]):
            hit = slot == lane_i + r * PTS
            tb[0][r:r + 1, :] = jnp.sum(jnp.where(hit, code, 0), axis=0, keepdims=True) - 1

    def links(chunks):
        for h, (kind, i) in enumerate(chunks):
            if kind:
                pair_tab(i).wait_recv()
            row = (ptb if kind else tb)[i][pl.ds(me // 8, 1), :]
            tile[h] = jnp.broadcast_to(row, (PTS, PTS)).T
        sub_i = lax.broadcasted_iota(I32, (CAP, PTS), 0)
        lane_i = lax.broadcasted_iota(I32, (CAP, PTS), 1)
        newest = last[...]
        for h, (kind, i) in enumerate(chunks):
            c = i + kind * RING
            code = tile[h, pl.ds((me % 8) * CAP, CAP), :]
            valid = code >= 0
            target = jnp.where(valid, lax.bitwise_and(code, LEAF_DEV - 1), PTS)
            hit = target == lane_i
            run = valid & (sub_i > 0) & (target == pltpu.roll(target, 1, 0))
            prev = jnp.sum(jnp.where(hit, jnp.broadcast_to(newest, (CAP, PTS)), 0), axis=1, keepdims=True)
            prev = jnp.where(run, 0, prev)
            word = jnp.where(valid, code, 0) + prev * 1024 + run.astype(I32) * (1024 * 1024)
            rec[c] = jnp.sum(jnp.where(sub_i == lane_i, word, 0), axis=0, keepdims=True)
            new = jnp.max(jnp.where(hit, sub_i + c * CAP, 0), axis=0, keepdims=True)
            newest = jnp.where(new > 0, new, newest)
        last[...] = newest
        return chunks

    def link_out(c):
        return pltpu.make_async_copy(rec.at[c], srec.at[c], csem.at[c])

    def far_chunk(c, om, pts):
        def body(b, full):
            for u in range(8):
                k = b * 8 + u
                word = srec[c, 0, k]
                src = lax.bitwise_and(lax.shift_right_logical(word, 5), LEAF_DEV - 1)
                t = lax.bitwise_and(word, LEAF_DEV - 1)
                prev = lax.bitwise_and(lax.shift_right_logical(word, 10), 1023)
                run = lax.shift_right_logical(word, 20).astype(F32)
                p = pts[src]
                dist = None
                for d in range(3):
                    dx = xb[t, d] - p[d:d + 1]
                    dist = dx * dx if dist is None else dist + dx * dx
                kern = lax.rsqrt((dist + DELTA_SQ).astype(BF))
                r = lax.dot_general(om[src], kern, (((1,), (1,)), ((), ())), preferred_element_type=F32)
                full = r + chain[prev] + full * run
                chain[c * CAP + k] = full
            return full

        lax.fori_loop(0, CAP // 8, body, jnp.zeros((rows, PTS), F32))

    def prepare(part):
        lane8 = lax.broadcasted_iota(I32, (8, PTS), 0)

        def leaf(t, carry):
            sl = pl.ds(pl.multiple_of(t * PTS, PTS), PTS)
            raw = mb[0][t]
            c = raw - 0.5
            cx, cy, cz = c[0:1], c[1:2], c[2:3]
            q = cx * cx + cy * cy + cz * cz
            for d in range(3):
                xb[t, d] = jnp.broadcast_to(raw[d:d + 1], (PTS, PTS)).T

            def stack(r0, r1, r2, r3, r4):
                v = jnp.where(lane8 == 0, r0, 0.0)
                v = jnp.where(lane8 == 1, r1, v)
                v = jnp.where(lane8 == 2, r2, v)
                v = jnp.where(lane8 == 3, r3, v)
                return jnp.where(lane8 == 4, r4, v)

            a1, a2, a3 = split3(stack(cx, cy, cz, q, 1.0))
            b1, b2, b3 = split3(stack(-2.0 * cx, -2.0 * cy, -2.0 * cz, 1.0, q + DELTA_SQ))
            left = jnp.concatenate([a1, a1, a2, a2, a1, a3], axis=0)
            fx[sl, :] = left.T.astype(BF)
            fy[:, sl] = jnp.concatenate([b1, b2, b1, b2, b3, b1], axis=0).astype(BF)
            return carry

        lax.fori_loop(part * 8, part * 8 + 8, leaf, 0, unroll=2)

    def prepare_counts():
        ids = near_ids_ref[...] - me * LEAF_DEV
        sub_i = lax.broadcasted_iota(I32, (LEAF_DEV, LEAF_DEV), 0)
        cnt = jnp.zeros((LEAF_DEV, LEAF_DEV), F32)
        for e in range(ids.shape[0]):
            cnt = cnt + (ids[e:e + 1, :] == sub_i).astype(F32)
        cnt = cnt.T
        for t in range(LEAF_DEV):
            cntx[:, t * PTS:(t + 1) * PTS] = jnp.broadcast_to(cnt[:, t:t + 1], (LEAF_DEV, PTS))

    def prepare_merge():
        for t in range(LEAF_DEV):
            pick = (lax.broadcasted_iota(I32, (PTS, SK), 0) == skel_ref[t:t + 1, :]).astype(F32).astype(BF)
            part = interp_ref[t // CHILD, :, (t % CHILD) * SK:(t % CHILD + 1) * SK]
            et[t] = lax.dot_general(part, pick, (((1,), (1,)), ((), ())), preferred_element_type=F32).astype(BF)

    def near_part(strip, half):
        here = pl.ds(pl.multiple_of(strip * 256, 256), 256)
        acc = None
        for j in range(half * n // 2, (half + 1) * n // 2, JSTEP):
            d = jnp.dot(fx[here, :], fy[:, j:j + JSTEP], preferred_element_type=F32)
            k = lax.rsqrt(d.astype(BF))
            c0 = cntx[pl.ds(2 * strip, 1), j:j + JSTEP].astype(BF)
            c1 = cntx[pl.ds(2 * strip + 1, 1), j:j + JSTEP].astype(BF)
            k = jnp.concatenate([k[:PTS] * c0, k[PTS:] * c1], axis=0)
            r = lax.dot_general(om_flat[:, j:j + JSTEP], k, (((1,), (1,)), ((), ())), preferred_element_type=F32)
            acc = r if acc is None else acc + r
        if half == 0:
            near_ref[:, here] = acc
        else:
            near_ref[:, here] += acc

    near_work = [(st, h) for st in range(LEAF_DEV // 2) for h in range(2)]
    far_ready = []

    def do_near(m):
        for a, b in near_work[:m]:
            near_part(a, b)
        del near_work[:m]

    def do_far(m):
        for _ in range(min(m, len(far_ready))):
            kind, i = far_ready.pop(0)
            c = i + kind * RING
            if kind:
                pair_om(i).wait_recv()
                pair_pts(i).wait_recv()
            link_out(c).wait()
            far_chunk(c, (pbufs if kind else bufs)[i], (pmb if kind else mb)[i])

    for way in (0, 1):
        ring_pts(0, way).start()
        ring_om(0, 0, way).start()
    for sub in range(1, NSUB):
        for way in (0, 1):
            ring_om(0, sub, way).start()
    pair_pts(0).start()
    pair_om(0).start()
    make_table()
    last[...] = jnp.zeros((1, PTS), I32)
    chain[0] = jnp.zeros((rows, PTS), F32)
    for way in (0, 1):
        ring_tab(0, way).start()
    pair_tab(0).start()

    for d in range(8):
        ways = [way for way in (0, 1) if small(d, way)]
        blocks = [ends(d, way)[1] for way in ways]
        arrived = [(kind, i) for kind in (0, 1) for i in blocks]
        if d == 0:
            arrived = [(1, 0)] + arrived
        if d < 7:
            events = [[(0, sub), (1, sub)] for sub in range(NSUB)]
        else:
            events = [[(0, sub), (1, sub + NSUB // 2)] for sub in range(NSUB // 2)]
        if d == 7:
            do_far(1)
        for e, event in enumerate(events):
            if e == 0:
                for way, i in zip(ways, blocks):
                    ring_pts(d, way).wait_recv()
                    if d < 7 and small(d + 1, way):
                        ring_pts(d + 1, way).start()
                    for k in range(1, n_probe):
                        probe_pts(i, k).start()
            for way, sub in event:
                i = ends(d, way)[1]
                ring_om(d, sub, way).wait_recv()
                if d < 7 and sub in subs(d + 1, way):
                    ring_om(d + 1, sub, way).start()
            if e == len(events) - 1:
                for i in blocks:
                    pair_om(i).start()
            if e == 0:
                for way, i in zip(ways, blocks):
                    ring_tab(d, way).wait_recv()
                    if d < 7 and small(d + 1, way):
                        ring_tab(d + 1, way).start()
                    pair_tab(i).start()
            if d == 0:
                prepare(2 * e)
                prepare(2 * e + 1)
            elif d < 7:
                do_near(2)
                do_far(3 if d == 1 and e == 1 else 2)
            else:
                do_far(1)
            if e == len(events) - 1:
                for i in blocks:
                    for k in range(1, n_probe):
                        probe_pts_in(i, k).wait_recv()
                    pair_pts(i).start()
        if d == 0:
            prepare_counts()
        links(arrived)
        if d < 7:
            do_near(2 if d == 0 else 1)
        else:
            do_far(1)
        for kind, i in arrived:
            link_out(i + kind * RING).start()
        if d == 0:
            prepare_merge()
        do_far(len(far_ready) if d == 7 else 0)
        far_ready += arrived
    last_out = pltpu.make_async_copy(last, slast, lsem)
    last_out.start()
    do_near(len(near_work))
    do_far(len(far_ready))
    last_out.wait()

    for p in range(LEAF_DEV // CHILD):
        m = None
        for t in range(p * CHILD, (p + 1) * CHILD):
            sl = slice(t * PTS, (t + 1) * PTS)
            v = near_ref[:, sl] + chain[slast[0, t]]
            near_ref[:, sl] = v
            r = lax.dot_general(v.astype(BF), et[t], (((1,), (1,)), ((), ())), preferred_element_type=F32)
            m = r if m is None else m + r
        merged[p] = m
        energy[p:p + 1] = jnp.broadcast_to(jnp.sum(m * m), (1, PTS))

    for d in range(8):
        for way in (0, 1):
            for sub in subs(d, way):
                ring_om(d, sub, way).wait_send()
            if small(d, way):
                i = ends(d, way)[1]
                ring_tab(d, way).wait_send()
                ring_pts(d, way).wait_send()
                for k in range(1, n_probe):
                    probe_pts(i, k).wait_send()
    copies = [
        remote(energy, got.at[k - 1], essem.at[k - 1], ersem.at[k - 1], me, (x + k) % n_probe) for k in range(1, n_probe)
    ]
    for cp in copies:
        cp.start()
    for i in range(RING):
        pair_om(i).wait_send()
        pair_tab(i).wait_send()
        pair_pts(i).wait_send()
    for cp in copies:
        cp.wait()
    total = energy[...]
    for k in range(n_probe - 1):
        total = total + got[k]
    factor = lax.rsqrt(total / (SK2 * rows * n_probe) + 1e-06)
    for p in range(LEAF_DEV // CHILD):
        parent_ref[:, p * SK2:(p + 1) * SK2] = merged[p] * factor[p:p + 1, :SK2]


def sample(om, coords, w, near_ids, far_pairs, skel, interp):
    rows, n = om.shape
    n_probe = lax.axis_size("probe")
    parents = LEAF_DEV // CHILD
    slots = 2 * RING * CAP
    dma = pltpu.SemaphoreType.DMA
    return pl.pallas_call(
        kernel_body,
        out_shape=(
            jax.ShapeDtypeStruct((rows, n), F32),
            jax.ShapeDtypeStruct((rows, parents * SK2), F32),
        ),
        in_specs=[VMEM] * 7,
        out_specs=(VMEM, VMEM),
        scratch_shapes=[pltpu.VMEM((LEAF_DEV, rows, PTS), BF)] * 32
        + [pltpu.VMEM((LEAF_DEV, 3, PTS), F32)] * 32
        + [pltpu.VMEM((RING * 2 * CAP // PTS, PTS), I32)] * 32
        + [
            pltpu.VMEM((rows, n), BF),
            pltpu.VMEM((2 * RING, 1, PTS), I32),
            pltpu.VMEM((1, PTS), I32),
            pltpu.VMEM((5, PTS, PTS), I32),
            pltpu.SMEM((2 * RING, 1, PTS), I32),
            pltpu.SMEM((1, PTS), I32),
            pltpu.VMEM((n, 48), BF),
            pltpu.VMEM((48, n), BF),
            pltpu.VMEM((LEAF_DEV, n), F32),
            pltpu.VMEM((LEAF_DEV, 3, PTS, PTS), F32),
            pltpu.VMEM((slots, rows, PTS), F32),
            pltpu.VMEM((LEAF_DEV, SK2, PTS), BF),
            pltpu.VMEM((parents, rows, SK2), F32),
            pltpu.VMEM((parents, PTS), F32),
            pltpu.VMEM((n_probe - 1, parents, PTS), F32),
            dma((2, 8, NSUB + 2)),
            dma((2, 8, NSUB + 2)),
            dma((RING, NSUB + 2)),
            dma((RING, NSUB + 2)),
            dma((RING, n_probe - 1)),
            dma((RING, n_probe - 1)),
            dma((2 * RING,)),
            dma(()),
            dma((n_probe - 1,)),
            dma((n_probe - 1,)),
        ],
        compiler_params=pltpu.CompilerParams(
            collective_id=0, has_side_effects=True, vmem_limit_bytes=62 * 1024 * 1024
        ),
        name="sample",
    )(om, coords, w, near_ids, far_pairs, skel, interp)


def per_device(coords, weights, omega, near_local, far_pairs, skel_rows, parent_interp):
    return sample(
        omega, coords, weights.reshape(1, -1), near_local.T, far_pairs, skel_rows, parent_interp.transpose(0, 2, 1)
    )


def solution(mesh):
    return jax.shard_map(
        per_device,
        mesh=mesh,
        in_specs=(
            P(None, "leaf"),
            P("leaf"),
            P("probe", "leaf"),
            P("leaf", None),
            P(None, "leaf"),
            P("leaf", None),
            P("leaf", None, None),
        ),
        out_specs=(P("probe", "leaf"), P("probe", "leaf")),
        check_vma=False,
    )
```
